32 devices in a mesh: cuts: 2 (over x), brick: 16 (over z, y, core).
Axes of the slice: x: 2, y: 2, z: 4, core: 2. Of those that a mesh axis runs over, the one named last changes fastest.
Arguments:
- eigen_vectors: float32 [64, 2, 3, 64, 512], P(None, None, None, ('cuts', 'brick')), parts along dimension 3, may hold values from -6 to 6
- link_field: float32 [3, 2, 3, 3, 64, 512], P(None, None, None, None, ('cuts', 'brick')), parts along dimension 4, may hold values from -3 to 3
- block_slot: int32 [63], replicated, may hold values from 0 to 63, as said below
Outputs:
- elementals: float32 [128, 32, 128], P(('cuts', 'brick')), parts along dimension 0
The draws below stay inside these ranges and needn't reach their ends.
There are 2 independent parts, one for each index of `cuts`. The reference program is written for one: setup_inputs(seed, part) draws one part's arguments, and reference() takes and returns one part's arrays. A program takes and returns all parts, laid end to end along the dimension named above; an argument that names none is the same for every part. Nothing has to cross between parts.
Inputs may be any that keep to these rules, and one draw needn't show every extreme that they name: block_slot names distinct slots; slot s belongs to device s // 4 of the brick axis; in every draw some device has all 4 of its slots named.
All inputs are finite; a program needn't handle non-finite values.
Results may differ from the reference program's by a relative error of at most 0.0044.
Values sent between devices are 32-bit elements; how exact they have to be, the bound alone decides.
A program may use at most 64 MiB of HBM per device.

```python
import math
import jax
import jax.numpy as jnp
import numpy as np
from jax import lax

NV = 64
PB = 32
CAP = 4
LX = 8
LY = 64
LZ = 32
NBLK = 63
SLOTS = 64


def draw_block_slot(key, part):
    key_owner, key_score, key_order = jax.random.split(key, 3)
    slot_ids = jnp.arange(SLOTS, dtype=jnp.int32)
    full_owner = jax.random.randint(key_owner, (), 0, SLOTS // CAP)
    slot_score = jax.random.permutation(key_score, SLOTS).astype(jnp.int32)
    slot_score = jnp.where(slot_ids // CAP == full_owner, slot_ids % CAP - CAP, slot_score)
    slot_order = jnp.argsort(slot_score, stable=True)[:NBLK]
    return jax.random.permutation(key_order, slot_order).astype(jnp.int32)


def block_scale(own_key, shape, cuts, low, high):
    level, own = 1.0, jax.random.fold_in(own_key, 6)
    for axis_at, shards_of in cuts:
        draws = jnp.exp(jax.random.uniform(jax.random.fold_in(own, axis_at), (shards_of,), jnp.float32, low / len(cuts), high / len(cuts)))
        level = level * jnp.repeat(draws, shape[axis_at] // shards_of).reshape([-1 if axis == axis_at else 1 for axis in range(len(shape))])
    return level


def centred(rng, shape, spread, limit, cuts=(), kind=jnp.bfloat16):
    array = jax.random.normal(rng, shape, jnp.float32) * spread
    if len(cuts) > 0:
        array = block_scale(rng, shape, cuts, -0.22, 0.18) * array
    return jnp.clip(array, min=-limit, max=limit).astype(kind)


def setup_inputs(seed: int = 0, part: int = 0) -> dict:
    splits = jax.random.split(jax.random.key(seed), 4)
    own_keys = jax.random.split(jax.random.fold_in(splits[3], part), 4)
    eigen_vectors = centred(own_keys[0], (NV, 2, 3, LZ, LX * LY), 1.0, 6.0, ((3, 16),), jnp.float32)
    link_field = centred(own_keys[1], (3, 2, 3, 3, LZ, LX * LY), 0.5, 3.0, ((4, 16),), jnp.float32)
    block_slot = draw_block_slot(jax.random.fold_in(splits[3], 71), part)
    return dict(eigen_vectors=eigen_vectors, link_field=link_field, block_slot=block_slot)


def periodic(lattice_field, rim_depth, along):
    plane_count = lattice_field.shape[along]
    lower = lax.slice_in_dim(lattice_field, plane_count - rim_depth, plane_count, axis=along)
    upper = lax.slice_in_dim(lattice_field, 0, rim_depth, axis=along)
    return jnp.concatenate([lower, lattice_field, upper], axis=along)

def shift_columns(lattice_field, forward):
    column = jnp.arange(lattice_field.shape[-1]) % LX
    if forward:
        return jnp.where(column == LX - 1, jnp.roll(lattice_field, LX - 1, axis=-1), jnp.roll(lattice_field, -1, axis=-1))
    return jnp.where(column == 0, jnp.roll(lattice_field, -(LX - 1), axis=-1), jnp.roll(lattice_field, 1, axis=-1))

def link_times(link_set, lattice_field):
    real_rows = []
    imag_rows = []
    for out_row in range(3):
        real_part = link_set[0, out_row, 0] * lattice_field[:, 0, 0] - link_set[1, out_row, 0] * lattice_field[:, 1, 0]
        imag_part = link_set[0, out_row, 0] * lattice_field[:, 1, 0] + link_set[1, out_row, 0] * lattice_field[:, 0, 0]
        for in_row in (1, 2):
            real_part = real_part + link_set[0, out_row, in_row] * lattice_field[:, 0, in_row] - link_set[1, out_row, in_row] * lattice_field[:, 1, in_row]
            imag_part = imag_part + link_set[0, out_row, in_row] * lattice_field[:, 1, in_row] + link_set[1, out_row, in_row] * lattice_field[:, 0, in_row]
        real_rows.append(real_part)
        imag_rows.append(imag_part)
    return jnp.stack([jnp.stack(real_rows, 1), jnp.stack(imag_rows, 1)], 1)

def adjoint_times(link_set, lattice_field):
    real_rows = []
    imag_rows = []
    for out_row in range(3):
        real_part = link_set[0, 0, out_row] * lattice_field[:, 0, 0] + link_set[1, 0, out_row] * lattice_field[:, 1, 0]
        imag_part = link_set[0, 0, out_row] * lattice_field[:, 1, 0] - link_set[1, 0, out_row] * lattice_field[:, 0, 0]
        for in_row in (1, 2):
            real_part = real_part + link_set[0, in_row, out_row] * lattice_field[:, 0, in_row] + link_set[1, in_row, out_row] * lattice_field[:, 1, in_row]
            imag_part = imag_part + link_set[0, in_row, out_row] * lattice_field[:, 1, in_row] - link_set[1, in_row, out_row] * lattice_field[:, 0, in_row]
        real_rows.append(real_part)
        imag_rows.append(imag_part)
    return jnp.stack([jnp.stack(real_rows, 1), jnp.stack(imag_rows, 1)], 1)

def apply_hops(lattice_field, link_field):
    inner_field = lattice_field[:, :, :, 1:-1]
    inner_links = link_field[:, :, :, :, 1:-1]
    hop_total = link_times(inner_links[0], shift_columns(inner_field, True))
    hop_total = hop_total + shift_columns(adjoint_times(inner_links[0], inner_field), False)
    hop_total = hop_total + link_times(inner_links[1], jnp.roll(inner_field, -LX, axis=4))
    hop_total = hop_total + jnp.roll(adjoint_times(inner_links[1], inner_field), LX, axis=4)
    hop_total = hop_total + link_times(link_field[2][:, :, :, 1:-1], lattice_field[:, :, :, 2:])
    hop_total = hop_total + adjoint_times(link_field[2][:, :, :, :-2], lattice_field[:, :, :, :-2])
    return hop_total * (1.0 / 6.0)

def diquark_block(left_rows, right_rows):
    real_rows = []
    imag_rows = []
    for colour in range(3):
        first_colour = (colour + 1) % 3
        second_colour = (colour + 2) % 3
        real_part = left_rows[:, 0, first_colour] * right_rows[:, 0, second_colour] - left_rows[:, 1, first_colour] * right_rows[:, 1, second_colour] - (left_rows[:, 0, second_colour] * right_rows[:, 0, first_colour] - left_rows[:, 1, second_colour] * right_rows[:, 1, first_colour])
        imag_part = left_rows[:, 0, first_colour] * right_rows[:, 1, second_colour] + left_rows[:, 1, first_colour] * right_rows[:, 0, second_colour] - (left_rows[:, 0, second_colour] * right_rows[:, 1, first_colour] + left_rows[:, 1, second_colour] * right_rows[:, 0, first_colour])
        real_rows.append(real_part)
        imag_rows.append(imag_part)
    return jnp.stack([jnp.stack(real_rows, 1), jnp.stack(imag_rows, 1)], 1)

def elemental_block(quarks, vectors_low):
    pair_count = quarks.shape[0]
    vector_count = vectors_low.shape[0]
    left_mat = quarks.astype(jnp.float32).reshape(pair_count * 2, -1)
    right_mat = vectors_low.astype(jnp.float32).reshape(vector_count * 2, -1)
    products = lax.dot_general(left_mat, right_mat, (((1,), (1,)), ((), ())), precision=lax.Precision.HIGHEST, preferred_element_type=jnp.float32)
    products = products.reshape(pair_count, 2, vector_count, 2)
    real_part = products[:, 0, :, 0] - products[:, 1, :, 1]
    imag_part = products[:, 0, :, 1] + products[:, 1, :, 0]
    return jnp.stack([real_part, imag_part], 1).reshape(pair_count, 2 * vector_count)

def reference(eigen_vectors, link_field, block_slot):
    link_wide = periodic(link_field, 1, 4)
    first_step = apply_hops(periodic(eigen_vectors, 1, 3), link_wide)
    filtered = 2.0 * apply_hops(periodic(first_step, 1, 3), link_wide) - eigen_vectors
    vectors_low = filtered.astype(jnp.bfloat16)
    first_index, second_index = np.triu_indices(NV, 1)
    first_table = jnp.asarray(first_index.reshape(NBLK, PB).astype(np.int32))
    second_table = jnp.asarray(second_index.reshape(NBLK, PB).astype(np.int32))

    def one_block(pair_rows):
        quarks = diquark_block(jnp.take(filtered, pair_rows[0], axis=0), jnp.take(filtered, pair_rows[1], axis=0)).astype(jnp.bfloat16)
        return elemental_block(quarks, vectors_low)
    blocks = lax.map(one_block, (first_table, second_table))
    factor = 1.0 / math.sqrt(3.0 * LX * LY * LZ)
    elemental = blocks * factor
    return jnp.zeros((SLOTS, PB, 2 * NV), jnp.float32).at[block_slot].set(elemental)
```

```python
import functools
import math

import jax
import jax.numpy as jnp
from jax import lax
from jax.experimental import pallas as pl
from jax.experimental.pallas import tpu as pltpu
from jax.sharding import PartitionSpec as P

PB = 32
CAP = 4
LX = 8
LY = 64

LANES = 128
TILE = 8
GROUP = 16
AHEAD = 4
MESH = pl.DeviceIdType.MESH


def shifted_columns(row, column, forward):
    lanes = row.shape[-1]
    if forward:
        return jnp.where(
            column == LX - 1, pltpu.roll(row, LX - 1, 1), pltpu.roll(row, lanes - 1, 1)
        )
    return jnp.where(column == 0, pltpu.roll(row, lanes - LX + 1, 1), pltpu.roll(row, 1, 1))


def times_link(links, field, adjoint, totals):
    for row in range(3):
        for col in range(3):
            at = col * 3 + row if adjoint else row * 3 + col
            real, imag = links(at), links(9 + at)
            if adjoint:
                terms = (
                    real * field[col] + imag * field[3 + col],
                    real * field[3 + col] - imag * field[col],
                )
            else:
                terms = (
                    real * field[col] - imag * field[3 + col],
                    real * field[3 + col] + imag * field[col],
                )
            for part, term in zip((row, 3 + row), terms):
                totals[part] = term if totals[part] is None else totals[part] + term


def pair_diquarks(left, right):
    parts = [None] * 6
    for colour in range(3):
        first = (colour + 1) % 3
        second = (colour + 2) % 3
        common = left[6 + first] * right[second] - left[6 + second] * right[first]
        turned = left[first] * right[3 + second] - left[second] * right[3 + first]
        summed = left[3 + first] * right[6 + second] - left[3 + second] * right[6 + first]
        parts[colour] = common - summed
        parts[3 + colour] = common + turned
    return parts


ROW_TILE = 8
DOT_TILES = 40


def row_tiles(vectors):
    tiles = []
    row_starts = []
    for left in range(vectors - 1):
        lowest = (left + 1) // ROW_TILE
        row_starts.append((len(tiles) - lowest) * ROW_TILE)
        tiles += [(left, tile) for tile in range(lowest, vectors // ROW_TILE)]
    return tiles, row_starts


def bit_orders(levels):
    plain = list(range(levels))
    return [plain, plain] + [plain[:1] + plain[2:] + plain[1:2]] * 2


def whole_kernel(factor, slot_ref, eigen_ref, link_ref, out_ref, *scratch):
    levels = lax.axis_size("brick").bit_length() - 1
    (
        first_ref,
        near_halo,
        far_halo,
        lower_ref,
        wide_ref,
        field_ref,
        mixed_ref,
        quark_ref,
        low_ref,
        sum_ref,
        pair_ref,
        inverse_ref,
        halo_send,
        halo_recv,
        link_send,
        link_recv,
        piece_send,
        piece_recv,
        *stages,
    ) = scratch
    held = stages[:levels]
    landed = stages[levels:]

    planes, chunks, _, vectors, _ = eigen_ref.shape
    count = lax.axis_size("brick")
    me = lax.axis_index("brick")
    above = lax.rem(me + 1, count)
    below = lax.rem(me + count - 1, count)
    bits = [lax.rem(me // (1 << level), 2) for level in range(levels)]
    partners = [me + (1 - 2 * bits[level]) * (1 << level) for level in range(levels)]

    barrier = pltpu.get_barrier_semaphore()
    for other in [below, above] + partners:
        pl.semaphore_signal(barrier, inc=1, device_id={"brick": other}, device_id_type=MESH)
    pl.semaphore_wait(barrier, 2 + levels)

    groups = vectors // GROUP

    def halo_copy(hop, side, chunk, group):
        source = (eigen_ref, first_ref)[hop]
        target = (near_halo, far_halo)[hop]
        rows = pl.ds(pl.multiple_of(group * GROUP, GROUP), GROUP)
        return pltpu.make_async_remote_copy(
            src_ref=source.at[planes - 1 if side == 0 else 0, chunk, :, rows],
            dst_ref=target.at[side, chunk, :, rows],
            send_sem=halo_send.at[hop, side, chunk, group],
            recv_sem=halo_recv.at[hop, side, chunk, group],
            device_id={"brick": above if side == 0 else below},
            device_id_type=MESH,
        )

    link_copy = pltpu.make_async_remote_copy(
        src_ref=link_ref.at[2, planes - 1],
        dst_ref=lower_ref,
        send_sem=link_send,
        recv_sem=link_recv,
        device_id={"brick": above},
        device_id_type=MESH,
    )
    link_copy.start()
    for piece in range(AHEAD):
        for side in range(2):
            halo_copy(0, side, piece // groups, piece % groups).start()

    def widen(direction, plane, block):
        for at in range(18):
            for chunk in range(chunks):
                wide_ref[direction, plane, chunk, at] = jnp.broadcast_to(
                    block[at : at + 1, chunk * LANES : (chunk + 1) * LANES], (TILE, LANES)
                )

    link_column = lax.broadcasted_iota(jnp.int32, link_ref.shape[2:], 1) % LX
    for plane in range(planes):
        along_x, along_y, along_z = (link_ref[axis, plane] for axis in range(3))
        widen(0, plane, along_x)
        widen(1, plane, shifted_columns(along_x, link_column, False))
        widen(2, plane, along_y)
        widen(3, plane, pltpu.roll(along_y, LX, 1))
        widen(4, plane, along_z)
        if plane > 0:
            widen(5, plane, link_ref[2, plane - 1])

    blocks = slot_ref.shape[0]
    slot_total = CAP * count

    def find_slot(slot, carry):
        def look(block, found):
            return jnp.where(slot_ref[block] == slot, block, found)

        inverse_ref[slot] = lax.fori_loop(0, blocks, look, blocks, unroll=True)
        return carry

    lax.fori_loop(0, slot_total, find_slot, 0)
    sum_ref[...] = jnp.zeros_like(sum_ref)

    link_copy.wait_recv()
    widen(5, 0, lower_ref[...])

    lane = lax.broadcasted_iota(jnp.int32, (TILE, LANES), 1)
    column = lane % LX

    def hop_tile(source, halo, chunk, plane, at):
        rows = pl.ds(pl.multiple_of(at * TILE, TILE), TILE)
        after = lax.rem(chunk + 1, chunks)
        before = lax.rem(chunk + chunks - 1, chunks)
        middle = [source[plane, chunk, part, rows, :] for part in range(6)]
        totals = [None] * 6

        def links(direction):
            return lambda at: wide_ref[direction, plane, chunk, at]

        field = [shifted_columns(cell, column, True) for cell in middle]
        times_link(links(0), field, False, totals)
        field = [shifted_columns(cell, column, False) for cell in middle]
        times_link(links(1), field, True, totals)
        field = [
            pltpu.roll(
                jnp.where(lane < LX, source[plane, after, part, rows, :], middle[part]),
                LANES - LX,
                1,
            )
            for part in range(6)
        ]
        times_link(links(2), field, False, totals)
        field = [
            pltpu.roll(
                jnp.where(lane < LANES - LX, middle[part], source[plane, before, part, rows, :]),
                LX,
                1,
            )
            for part in range(6)
        ]
        times_link(links(3), field, True, totals)
        if plane + 1 < planes:
            field = [source[plane + 1, chunk, part, rows, :] for part in range(6)]
        else:
            field = [halo[1, chunk, part, rows, :] for part in range(6)]
        times_link(links(4), field, False, totals)
        if plane > 0:
            field = [source[plane - 1, chunk, part, rows, :] for part in range(6)]
        else:
            field = [halo[0, chunk, part, rows, :] for part in range(6)]
        times_link(links(5), field, True, totals)
        return rows, [total * (1.0 / 6.0) for total in totals]

    steps = chunks * groups

    def first_piece(step, carry):
        chunk, group = step // groups, lax.rem(step, groups)
        for side in range(2):
            halo_copy(0, side, chunk, group).wait_recv()

        @pl.when(step + AHEAD < steps)
        def _():
            later = step + AHEAD
            for side in range(2):
                halo_copy(0, side, later // groups, lax.rem(later, groups)).start()

        def one_tile(at, inner):
            for plane in range(planes):
                rows, values = hop_tile(eigen_ref, near_halo, chunk, plane, at)
                for part in range(6):
                    first_ref[plane, chunk, part, rows, :] = values[part]
            return inner

        lax.fori_loop(group * (GROUP // TILE), (group + 1) * (GROUP // TILE), one_tile, 0)
        for side in range(2):
            halo_copy(1, side, chunk, group).start()
        return carry

    tiles, row_starts = row_tiles(vectors)

    def elementals(plane, carry):
        for colour in range(3):
            real = field_ref[plane, colour]
            imag = field_ref[plane, 3 + colour]
            mixed_ref[colour] = imag - real
            mixed_ref[3 + colour] = imag + real
            real_low = real.astype(jnp.bfloat16)
            imag_low = imag.astype(jnp.bfloat16)
            real_at = slice(colour * LANES, (colour + 1) * LANES)
            imag_at = slice((3 + colour) * LANES, (4 + colour) * LANES)
            low_ref[:vectors, real_at] = real_low
            low_ref[:vectors, imag_at] = -imag_low
            low_ref[vectors:, real_at] = imag_low
            low_ref[vectors:, imag_at] = real_low

        lefts = {}

        def one_tile(left_at, tile):
            rows = slice(tile * ROW_TILE, (tile + 1) * ROW_TILE)

            def spread(cells):
                return jnp.broadcast_to(cells, (ROW_TILE, LANES))

            if left_at not in lefts:
                lefts.clear()
                at = slice(left_at, left_at + 1)
                left = [spread(field_ref[plane, part, at, :]) for part in range(6)]
                left += [spread(mixed_ref[3 + colour, at, :]) for colour in range(3)]
                lefts[left_at] = left
            left = lefts[left_at]
            right = [field_ref[plane, colour, rows, :] for colour in range(3)]
            right += [mixed_ref[part, rows, :] for part in range(6)]
            return pair_diquarks(left, right)

        for from_tile in range(0, len(tiles), DOT_TILES):
            to_tile = min(from_tile + DOT_TILES, len(tiles))
            for at in range(from_tile, to_tile, 2):
                upper = one_tile(*tiles[at])
                lower = one_tile(*tiles[at + 1])
                for part in range(6):
                    quark_ref[
                        at * ROW_TILE : (at + 2) * ROW_TILE, part * LANES : (part + 1) * LANES
                    ] = jnp.concatenate([upper[part], lower[part]], 0).astype(jnp.bfloat16)
            rows = slice(from_tile * ROW_TILE, to_tile * ROW_TILE)
            sum_ref[rows, :] += lax.dot_general(
                quark_ref[rows, :],
                low_ref[...],
                (((1,), (1,)), ((), ())),
                preferred_element_type=jnp.float32,
            )
        return carry

    def last_chunk(chunk, carry):
        def one_tile(at, inner):
            for plane in range(planes):
                rows, values = hop_tile(first_ref, far_halo, chunk, plane, at)
                for part in range(6):
                    field_ref[plane, part, rows, :] = (
                        2.0 * values[part] - eigen_ref[plane, chunk, part, rows, :]
                    )
            return inner

        def one_group(group, inner):
            for side in range(2):
                halo_copy(1, side, chunk, group).wait_recv()
            tiles_in = GROUP // TILE
            return lax.fori_loop(group * tiles_in, (group + 1) * tiles_in, one_tile, inner)

        lax.fori_loop(0, groups, one_group, 0)
        lax.fori_loop(0, planes, elementals, 0)
        return carry

    lax.fori_loop(0, steps, first_piece, 0)
    lax.fori_loop(0, chunks, last_chunk, 0)

    pair_at = 0
    for left in range(vectors - 1):
        rows = vectors - 1 - left
        start = row_starts[left] + left + 1
        done = 0
        while done < rows:
            block, row = divmod(pair_at + done, PB)
            some = min(PB - row, rows - done)
            from_row = start + done
            pair_ref[block, row : row + some, :] = sum_ref[from_row : from_row + some, :] * factor
            done += some
        pair_at += rows
    pair_ref[blocks] = jnp.zeros((PB, 2 * vectors), jnp.float32)

    orders = bit_orders(levels)

    def piece_copy(level, piece):
        axis = orders[piece][level]
        return pltpu.make_async_remote_copy(
            src_ref=held[level].at[piece, 1 - bits[axis]],
            dst_ref=landed[level].at[piece],
            send_sem=piece_send.at[level, piece],
            recv_sem=piece_recv.at[level, piece],
            device_id={"brick": partners[axis]},
            device_id_type=MESH,
        )

    schedule = [0, 2, 1, 3]
    for piece in schedule:
        for device in range(count):
            at = tuple((device >> axis) & 1 for axis in orders[piece])
            held[0][(piece,) + at] = pair_ref[inverse_ref[device * CAP + piece]]
        piece_copy(0, piece).start()
    for level in range(levels):
        for piece in schedule:
            piece_copy(level, piece).wait_recv()
            total = held[level][piece, bits[orders[piece][level]]] + landed[level][piece]
            if level + 1 < levels:
                held[level + 1][piece] = total
                piece_copy(level + 1, piece).start()
            else:
                out_ref[piece] = total
    link_copy.wait_send()
    for hop in range(2):
        for chunk in range(chunks):
            for group in range(groups):
                for side in range(2):
                    halo_copy(hop, side, chunk, group).wait_send()
    for level in range(levels):
        for piece in schedule:
            piece_copy(level, piece).wait_send()


def elementals_of(eigen, links, block_slot, factor):
    planes, chunks, parts, vectors, lanes = eigen.shape
    devices = lax.axis_size("brick")
    levels = devices.bit_length() - 1
    tile_rows = len(row_tiles(vectors)[0]) * ROW_TILE
    halo = pltpu.VMEM((2, chunks, parts, vectors, lanes), jnp.float32)
    vmem = pl.BlockSpec(memory_space=pltpu.VMEM)
    copies = pltpu.SemaphoreType.DMA((2, 2, chunks, vectors // GROUP))
    pieces = pltpu.SemaphoreType.DMA((levels, CAP))

    def stage(depth):
        return pltpu.VMEM((CAP,) + (2,) * depth + (PB, 2 * vectors), jnp.float32)

    return pl.pallas_call(
        functools.partial(whole_kernel, factor),
        in_specs=[pl.BlockSpec(memory_space=pltpu.SMEM), vmem, vmem],
        out_specs=vmem,
        out_shape=jax.ShapeDtypeStruct((CAP, PB, 2 * vectors), jnp.float32),
        scratch_shapes=[
            pltpu.VMEM(eigen.shape, jnp.float32),
            halo,
            halo,
            pltpu.VMEM(links.shape[2:], jnp.float32),
            pltpu.VMEM((6, planes, chunks, 18, TILE, lanes), jnp.float32),
            pltpu.VMEM((planes, 6, vectors, lanes), jnp.float32),
            pltpu.VMEM((6, vectors, lanes), jnp.float32),
            pltpu.VMEM((tile_rows, 6 * lanes), jnp.bfloat16),
            pltpu.VMEM((2 * vectors, 6 * lanes), jnp.bfloat16),
            pltpu.VMEM((tile_rows, 2 * vectors), jnp.float32),
            pltpu.VMEM((block_slot.shape[0] + 1, PB, 2 * vectors), jnp.float32),
            pltpu.SMEM((CAP * devices,), jnp.int32),
            copies,
            copies,
            pltpu.SemaphoreType.DMA,
            pltpu.SemaphoreType.DMA,
            pieces,
            pieces,
        ]
        + [stage(levels - level) for level in range(levels)]
        + [stage(levels - 1 - level) for level in range(levels)],
        compiler_params=pltpu.CompilerParams(
            collective_id=0, has_side_effects=True, vmem_limit_bytes=44 << 20
        ),
        name="elementals",
    )(block_slot, eigen, links)


def on_device(eigen_vectors, link_field, block_slot):
    vectors = eigen_vectors.shape[0]
    planes, sites = eigen_vectors.shape[3:]
    chunks = sites // LANES
    eigen = eigen_vectors.reshape(vectors, 6, planes, chunks, LANES)
    eigen = jnp.transpose(eigen, (2, 3, 1, 0, 4))
    links = jnp.transpose(link_field, (0, 4, 1, 2, 3, 5)).reshape(3, planes, 18, sites)
    factor = 1.0 / math.sqrt(3.0 * LX * LY * planes * lax.axis_size("brick"))
    return elementals_of(eigen, links, block_slot, factor)


def solution(mesh):
    return jax.shard_map(
        on_device,
        mesh=mesh,
        in_specs=(
            P(None, None, None, ("cuts", "brick"), None),
            P(None, None, None, None, ("cuts", "brick"), None),
            P(),
        ),
        out_specs=P(("cuts", "brick"), None, None),
        check_vma=False,
    )
```

```python
import functools
import math

import jax
import jax.numpy as jnp
from jax import lax
from jax.experimental import pallas as pl
from jax.experimental.pallas import tpu as pltpu
from jax.sharding import PartitionSpec as P

PB = 32
CAP = 4
LX = 8
LY = 64

LANES = 128
TILE = 8
GROUP = 32
ROWS = 16
AHEAD = 2
MESH = pl.DeviceIdType.MESH


def shifted_columns(row, column, forward):
    lanes = row.shape[-1]
    if forward:
        return jnp.where(
            column == LX - 1, pltpu.roll(row, LX - 1, 1), pltpu.roll(row, lanes - 1, 1)
        )
    return jnp.where(column == 0, pltpu.roll(row, lanes - LX + 1, 1), pltpu.roll(row, 1, 1))


def times_link(links, field, adjoint, totals):
    for row in range(3):
        for col in range(3):
            at = col * 3 + row if adjoint else row * 3 + col
            real, imag = links(at), links(9 + at)
            if adjoint:
                terms = (
                    real * field[col] + imag * field[3 + col],
                    real * field[3 + col] - imag * field[col],
                )
            else:
                terms = (
                    real * field[col] - imag * field[3 + col],
                    real * field[3 + col] + imag * field[col],
                )
            for part, term in zip((row, 3 + row), terms):
                totals[part] = term if totals[part] is None else totals[part] + term


def pair_diquarks(left, right):
    parts = [None] * 6
    for colour in range(3):
        first = (colour + 1) % 3
        second = (colour + 2) % 3
        common = left[6 + first] * right[second] - left[6 + second] * right[first]
        turned = left[first] * right[3 + second] - left[second] * right[3 + first]
        summed = left[3 + first] * right[6 + second] - left[3 + second] * right[6 + first]
        parts[colour] = common - summed
        parts[3 + colour] = common + turned
    return parts


ROW_TILE = 8
DOT_TILES = 32


def row_tiles(half):
    tiles = []
    count = half // ROW_TILE
    for side in range(2):
        for left in range(half - ROW_TILE):
            tiles += [(side, left, tile, 0) for tile in range(left // ROW_TILE + 1, count)]
        for tile in range(count):
            for shift in range(1, ROW_TILE // 2 + 1):
                tiles.append((side, None, tile, shift))
    return tiles


def stage_order(chunks):
    order = [(0, chunk) for chunk in range(min(3, chunks))]
    for chunk in range(3, chunks):
        order += [(1, chunk - 2), (0, chunk)]
    left = [chunk for chunk in range(chunks) if (1, chunk) not in order]
    return order + [(1, chunk) for chunk in left if chunk > 0] + [(1, 0)]


def bit_orders(levels):
    plain = list(range(levels))
    return [plain, plain] + [plain[:1] + plain[2:3] + plain[1:2] + plain[3:]] * 2


def whole_kernel(factor, slot_ref, eigen_in, link_in, out_ref, *scratch):
    levels = lax.axis_size("brick").bit_length() - 1
    (
        eigen_ref,
        link_ref,
        first_ref,
        near_halo,
        far_halo,
        lower_ref,
        wide_ref,
        field_ref,
        mixed_ref,
        quark_ref,
        low_ref,
        sum_ref,
        square_ref,
        turned_ref,
        pair_ref,
        inverse_ref,
        eigen_load,
        link_load,
        halo_send,
        halo_recv,
        link_send,
        link_recv,
        piece_send,
        piece_recv,
        *stages,
    ) = scratch
    held = stages[:levels]
    landed = stages[levels:]

    planes, chunks, _, vectors, _ = eigen_ref.shape
    count = lax.axis_size("brick")
    me = lax.axis_index("brick")
    above = lax.rem(me + 1, count)
    below = lax.rem(me + count - 1, count)
    bits = [lax.rem(me // (1 << level), 2) for level in range(levels)]
    partners = [me + (1 - 2 * bits[level]) * (1 << level) for level in range(levels)]

    barrier = pltpu.get_barrier_semaphore()
    for other in [below, above] + partners:
        pl.semaphore_signal(barrier, inc=1, device_id={"brick": other}, device_id_type=MESH)

    def load_links(axis, plane):
        return pltpu.make_async_copy(
            link_in.at[axis, :, plane], link_ref.at[axis, plane], link_load.at[axis, plane]
        )

    def load_eigen(plane, chunk, part):
        return pltpu.make_async_copy(
            eigen_in.at[:, part, plane, pl.ds(chunk * LANES, LANES)],
            eigen_ref.at[plane, chunk, part],
            eigen_load.at[plane, chunk, part],
        )

    axis_planes = [(axis, plane) for axis in (2, 0, 1) for plane in reversed(range(planes))]

    def start_eigen(chunk):
        for plane in range(planes):
            for part in range(6):
                load_eigen(plane, chunk, part).start()

    start_eigen(0)
    load_links(*axis_planes[0]).start()

    def wait_eigen(chunk):
        for plane in range(planes):
            for part in range(6):
                load_eigen(plane, chunk, part).wait()

    pl.semaphore_wait(barrier, 2 + levels)

    groups = vectors // GROUP

    def halo_copy(hop, side, chunk, group):
        source = (eigen_ref, first_ref)[hop]
        target = (near_halo, far_halo)[hop]
        rows = pl.ds(pl.multiple_of(group * GROUP, GROUP), GROUP)
        return pltpu.make_async_remote_copy(
            src_ref=source.at[planes - 1 if side == 0 else 0, chunk, :, rows],
            dst_ref=target.at[side, chunk, :, rows],
            send_sem=halo_send.at[hop, side, chunk, group],
            recv_sem=halo_recv.at[hop, side, chunk, group],
            device_id={"brick": above if side == 0 else below},
            device_id_type=MESH,
        )

    link_copy = pltpu.make_async_remote_copy(
        src_ref=link_ref.at[2, planes - 1],
        dst_ref=lower_ref,
        send_sem=link_send,
        recv_sem=link_recv,
        device_id={"brick": above},
        device_id_type=MESH,
    )
    order = stage_order(chunks)

    def stage_of(stage):
        hop, chunk = order[-1]
        for at, (other_hop, other_chunk) in enumerate(order[:-1]):
            hop = jnp.where(stage == at, other_hop, hop)
            chunk = jnp.where(stage == at, other_chunk, chunk)
        return hop, chunk

    for at, (hop, chunk) in enumerate(order[:AHEAD]):
        wait_eigen(chunk)
        for group in range(groups):
            for side in range(2):
                halo_copy(hop, side, chunk, group).start()
        if at == 0:
            load_links(2, planes - 1).wait()
            link_copy.start()
            for later in range(1, chunks):
                start_eigen(later)
            for axis, plane in axis_planes[1:]:
                load_links(axis, plane).start()

    for axis, plane in axis_planes[1:]:
        load_links(axis, plane).wait()
    for hop, chunk in order[AHEAD:]:
        if hop == 0:
            wait_eigen(chunk)

    def widen(direction, plane, block):
        for at in range(18):
            for chunk in range(chunks):
                wide_ref[direction, plane, chunk, at] = jnp.broadcast_to(
                    block[at : at + 1, chunk * LANES : (chunk + 1) * LANES], (TILE, LANES)
                )

    link_column = lax.broadcasted_iota(jnp.int32, link_ref.shape[2:], 1) % LX
    for plane in range(planes):
        along_x, along_y, along_z = (link_ref[axis, plane] for axis in range(3))
        widen(0, plane, along_x)
        widen(1, plane, shifted_columns(along_x, link_column, False))
        widen(2, plane, along_y)
        widen(3, plane, pltpu.roll(along_y, LX, 1))
        widen(4, plane, along_z)
        if plane > 0:
            widen(5, plane, link_ref[2, plane - 1])

    blocks = slot_ref.shape[0]
    slot_total = CAP * count

    def find_slot(slot, carry):
        def look(block, found):
            return jnp.where(slot_ref[block] == slot, block, found)

        inverse_ref[slot] = lax.fori_loop(0, blocks, look, blocks, unroll=True)
        return carry

    lax.fori_loop(0, slot_total, find_slot, 0)
    sum_ref[...] = jnp.zeros_like(sum_ref)

    link_copy.wait_recv()
    widen(5, 0, lower_ref[...])

    lane = lax.broadcasted_iota(jnp.int32, (ROWS, LANES), 1)
    column = lane % LX

    def hop_tile(source, halo, chunk, plane, at):
        rows = pl.ds(pl.multiple_of(at * ROWS, ROWS), ROWS)
        after = lax.rem(chunk + 1, chunks)
        before = lax.rem(chunk + chunks - 1, chunks)
        middle = [source[plane, chunk, part, rows, :] for part in range(6)]
        totals = [None] * 6

        def links(direction):
            def link(at):
                return jnp.concatenate([wide_ref[direction, plane, chunk, at]] * (ROWS // TILE), 0)

            return link

        field = [shifted_columns(cell, column, True) for cell in middle]
        times_link(links(0), field, False, totals)
        field = [shifted_columns(cell, column, False) for cell in middle]
        times_link(links(1), field, True, totals)
        field = [
            pltpu.roll(
                jnp.where(lane < LX, source[plane, after, part, rows, :], middle[part]),
                LANES - LX,
                1,
            )
            for part in range(6)
        ]
        times_link(links(2), field, False, totals)
        field = [
            pltpu.roll(
                jnp.where(lane < LANES - LX, middle[part], source[plane, before, part, rows, :]),
                LX,
                1,
            )
            for part in range(6)
        ]
        times_link(links(3), field, True, totals)
        if plane + 1 < planes:
            field = [source[plane + 1, chunk, part, rows, :] for part in range(6)]
        else:
            field = [halo[1, chunk, part, rows, :] for part in range(6)]
        times_link(links(4), field, False, totals)
        if plane > 0:
            field = [source[plane - 1, chunk, part, rows, :] for part in range(6)]
        else:
            field = [halo[0, chunk, part, rows, :] for part in range(6)]
        times_link(links(5), field, True, totals)
        return rows, totals

    tiles_in = GROUP // ROWS

    def send_later(stage, group):
        for hop in range(2):
            later_hop, later_chunk = stage_of(stage + AHEAD)

            @pl.when(jnp.logical_and(stage + AHEAD < len(order), later_hop == hop))
            def _():
                for side in range(2):
                    halo_copy(hop, side, later_chunk, group).start()

    def first_stage(stage, chunk):
        def one_group(group, carry):
            for side in range(2):
                halo_copy(0, side, chunk, group).wait_recv()

            def one_tile(at, inner):
                for plane in range(planes):
                    rows, values = hop_tile(eigen_ref, near_halo, chunk, plane, at)
                    for part in range(6):
                        first_ref[plane, chunk, part, rows, :] = values[part] * (1.0 / 6.0)
                return inner

            for at in range(tiles_in):
                one_tile(group * tiles_in + at, 0)
            send_later(stage, group)
            return carry

        lax.fori_loop(0, groups, one_group, 0)

    half = vectors // 2
    tiles = row_tiles(half)

    def elementals(plane, carry):
        for colour in range(3):
            real = field_ref[plane, colour]
            imag = field_ref[plane, 3 + colour]
            mixed_ref[colour] = imag - real
            mixed_ref[3 + colour] = imag + real
            real_low = real.astype(jnp.bfloat16)
            imag_low = imag.astype(jnp.bfloat16)
            real_at = slice(colour * LANES, (colour + 1) * LANES)
            imag_at = slice((3 + colour) * LANES, (4 + colour) * LANES)
            low_ref[:vectors, real_at] = real_low
            low_ref[:vectors, imag_at] = -imag_low
            low_ref[vectors:, real_at] = imag_low
            low_ref[vectors:, imag_at] = real_low

        lefts = {}

        def one_tile(side, left_at, tile, shift):
            rows = slice(side * half + tile * ROW_TILE, side * half + (tile + 1) * ROW_TILE)
            right = [field_ref[plane, colour, rows, :] for colour in range(3)]
            right += [mixed_ref[part, rows, :] for part in range(6)]
            if left_at is None:
                left = [field_ref[plane, part, rows, :] for part in range(6)] + right[6:]
                right = [pltpu.roll(cells, ROW_TILE - shift, 0) for cells in right]
                return pair_diquarks(left, right)
            left_at += side * half

            def spread(cells):
                return jnp.broadcast_to(cells, (ROW_TILE, LANES))

            if left_at not in lefts:
                lefts.clear()
                at = slice(left_at, left_at + 1)
                left = [spread(field_ref[plane, part, at, :]) for part in range(6)]
                left += [spread(mixed_ref[3 + colour, at, :]) for colour in range(3)]
                lefts[left_at] = left
            left = lefts[left_at]
            return pair_diquarks(left, right)

        for from_tile in range(0, len(tiles), DOT_TILES):
            to_tile = min(from_tile + DOT_TILES, len(tiles))
            for at in range(from_tile, to_tile, 2):
                upper = one_tile(*tiles[at])
                lower = one_tile(*tiles[at + 1])
                for part in range(6):
                    quark_ref[
                        at * ROW_TILE : (at + 2) * ROW_TILE, part * LANES : (part + 1) * LANES
                    ] = jnp.concatenate([upper[part], lower[part]], 0).astype(jnp.bfloat16)
            rows = slice(from_tile * ROW_TILE, to_tile * ROW_TILE)
            sum_ref[rows, :] += lax.dot_general(
                quark_ref[rows, :],
                low_ref[...],
                (((1,), (1,)), ((), ())),
                preferred_element_type=jnp.float32,
            )
        return carry

    def last_stage(stage, chunk):
        def one_group(group, carry):
            for side in range(2):
                halo_copy(1, side, chunk, group).wait_recv()
            send_later(stage, group)

            def one_tile(at, inner):
                for plane in range(planes):
                    rows, values = hop_tile(first_ref, far_halo, chunk, plane, at)
                    for part in range(6):
                        field_ref[plane, part, rows, :] = (
                            (1.0 / 3.0) * values[part] - eigen_ref[plane, chunk, part, rows, :]
                        )
                return inner

            for at in range(tiles_in):
                one_tile(group * tiles_in + at, 0)
            return carry

        lax.fori_loop(0, groups, one_group, 0)
        lax.fori_loop(0, planes, elementals, 0)

    def one_stage(stage, carry):
        hop, chunk = stage_of(stage)

        @pl.when(hop == 0)
        def _():
            first_stage(stage, chunk)

        @pl.when(hop == 1)
        def _():
            last_stage(stage, chunk)

        return carry

    lax.fori_loop(0, len(order), one_stage, 0)

    def put_pairs(pair_at, cells):
        done = 0
        while done < cells.shape[0]:
            block, row = divmod(pair_at + done, PB)
            some = min(PB - row, cells.shape[0] - done)
            pair_ref[block, row : row + some, :] = cells[done : done + some]
            done += some

    def first_pair(left):
        return left * (2 * vectors - left - 1) // 2

    def square_rows(side, left, row, rows):
        start = (side * half + left) * half + row
        return slice(start, start + rows)

    def square_put(side, left, row, cells, left_step, row_step):
        start = (side * half + left) * half + row
        step = left_step * half + row_step
        square_ref[pl.ds(start, cells.shape[0], stride=step), :] = cells

    for at, (side, left, tile, shift) in enumerate(tiles):
        cells = sum_ref[at * ROW_TILE : (at + 1) * ROW_TILE, :] * factor
        row = tile * ROW_TILE
        if shift == 0:
            square_ref[square_rows(side, left, row, ROW_TILE), :] = cells
            square_put(side, row, left, -cells, 1, 0)
        else:
            upper, lower = cells[: ROW_TILE - shift], cells[ROW_TILE - shift :]
            square_put(side, row, row + shift, upper, 1, 1)
            square_put(side, row + shift, row, -upper, 1, 1)
            square_put(side, row + ROW_TILE - shift, row, lower, 1, 1)
            square_put(side, row, row + ROW_TILE - shift, -lower, 1, 1)
    for side in range(2):
        for row in range(0, half, ROW_TILE):
            nothing = jnp.zeros((ROW_TILE, 2 * vectors), jnp.float32)
            square_put(side, row, row, nothing, 1, 1)
        for left in range(half - 1):
            rows = square_rows(side, left, left + 1, half - 1 - left)
            put_pairs(first_pair(side * half + left), square_ref[rows, :])

    together = 2 * vectors // half
    apart = half // together
    for at in range(apart):
        stack = [square_ref[square_rows(1, at + apart * up, 0, half), :] for up in range(together)]
        turned_ref[pl.ds(at, 2 * vectors, stride=apart), :] = jnp.concatenate(stack, 0).T
    part = lax.broadcasted_iota(jnp.int32, (half, 2 * vectors), 1) // half
    for quad in range(apart):
        mine = square_ref[square_rows(0, quad * together, 0, together * half), :].T
        near_real = -mine[half:vectors]
        near_imag = -mine[vectors + half :]
        for up in range(together):
            left = quad * together + up

            def far(row):
                cells = turned_ref[row * apart : (row + 1) * apart, :]
                return jnp.concatenate(
                    [
                        pltpu.roll(cells, (2 * half * (row >= vectors) + half - half * at) % LANES, 1)
                        for at in range(together)
                    ],
                    0,
                )

            def near(cells, to):
                return pltpu.roll(cells, (to - up) * half % LANES, 1)

            cells = jnp.where(part == 0, near(near_real, 0), near(near_imag, 2))
            cells = jnp.where(part == 1, far(left), cells)
            cells = jnp.where(part == 3, far(vectors + left), cells)
            put_pairs(first_pair(left) + half - 1 - left, cells)
    pair_ref[blocks] = jnp.zeros((PB, 2 * vectors), jnp.float32)

    orders = bit_orders(levels)

    def piece_copy(level, piece):
        axis = orders[piece][level]
        return pltpu.make_async_remote_copy(
            src_ref=held[level].at[piece, 1 - bits[axis]],
            dst_ref=landed[level].at[piece],
            send_sem=piece_send.at[level, piece],
            recv_sem=piece_recv.at[level, piece],
            device_id={"brick": partners[axis]},
            device_id_type=MESH,
        )

    schedule = [0, 2, 1, 3]
    for piece in schedule:
        for device in range(count):
            at = tuple((device >> axis) & 1 for axis in orders[piece])
            held[0][(piece,) + at] = pair_ref[inverse_ref[device * CAP + piece]]
        piece_copy(0, piece).start()
    for level in range(levels):
        for piece in schedule:
            piece_copy(level, piece).wait_recv()
            total = held[level][piece, bits[orders[piece][level]]] + landed[level][piece]
            if level + 1 < levels:
                held[level + 1][piece] = total
                piece_copy(level + 1, piece).start()
            else:
                out_ref[piece] = total
    link_copy.wait_send()
    for hop in range(2):
        for chunk in range(chunks):
            for group in range(groups):
                for side in range(2):
                    halo_copy(hop, side, chunk, group).wait_send()
    for level in range(levels):
        for piece in schedule:
            piece_copy(level, piece).wait_send()


def elementals_of(eigen, links, block_slot, factor):
    vectors, parts, planes, sites = eigen.shape
    chunks, lanes = sites // LANES, LANES
    devices = lax.axis_size("brick")
    levels = devices.bit_length() - 1
    tile_rows = len(row_tiles(vectors // 2)) * ROW_TILE
    halo = pltpu.VMEM((2, chunks, parts, vectors, lanes), jnp.float32)
    vmem = pl.BlockSpec(memory_space=pltpu.VMEM)
    stay = pl.BlockSpec(memory_space=pl.ANY)
    copies = pltpu.SemaphoreType.DMA((2, 2, chunks, vectors // GROUP))
    pieces = pltpu.SemaphoreType.DMA((levels, CAP))

    def stage(depth):
        return pltpu.VMEM((CAP,) + (2,) * depth + (PB, 2 * vectors), jnp.float32)

    return pl.pallas_call(
        functools.partial(whole_kernel, factor),
        in_specs=[pl.BlockSpec(memory_space=pltpu.SMEM), stay, stay],
        out_specs=vmem,
        out_shape=jax.ShapeDtypeStruct((CAP, PB, 2 * vectors), jnp.float32),
        scratch_shapes=[
            pltpu.VMEM((planes, chunks, parts, vectors, lanes), jnp.float32),
            pltpu.VMEM((3, planes, 18, sites), jnp.float32),
            pltpu.VMEM((planes, chunks, parts, vectors, lanes), jnp.float32),
            halo,
            halo,
            pltpu.VMEM((18, sites), jnp.float32),
            pltpu.VMEM((6, planes, chunks, 18, TILE, lanes), jnp.float32),
            pltpu.VMEM((planes, 6, vectors, lanes), jnp.float32),
            pltpu.VMEM((6, vectors, lanes), jnp.float32),
            pltpu.VMEM((tile_rows, 6 * lanes), jnp.bfloat16),
            pltpu.VMEM((2 * vectors, 6 * lanes), jnp.bfloat16),
            pltpu.VMEM((tile_rows, 2 * vectors), jnp.float32),
            pltpu.VMEM((vectors * vectors // 2, 2 * vectors), jnp.float32),
            pltpu.VMEM((vectors // 4 * vectors, 2 * vectors), jnp.float32),
            pltpu.VMEM((block_slot.shape[0] + 1, PB, 2 * vectors), jnp.float32),
            pltpu.SMEM((CAP * devices,), jnp.int32),
            pltpu.SemaphoreType.DMA((planes, chunks, 6)),
            pltpu.SemaphoreType.DMA((3, planes)),
            copies,
            copies,
            pltpu.SemaphoreType.DMA,
            pltpu.SemaphoreType.DMA,
            pieces,
            pieces,
        ]
        + [stage(levels - level) for level in range(levels)]
        + [stage(levels - 1 - level) for level in range(levels)],
        compiler_params=pltpu.CompilerParams(
            collective_id=0, has_side_effects=True, vmem_limit_bytes=60 << 20
        ),
        name="elementals",
    )(block_slot, eigen, links)


def on_device(eigen_vectors, link_field, block_slot):
    vectors = eigen_vectors.shape[0]
    planes, sites = eigen_vectors.shape[3:]
    eigen = eigen_vectors.reshape(vectors, 6, planes, sites)
    links = link_field.reshape(3, 18, planes, sites)
    factor = 1.0 / math.sqrt(3.0 * LX * LY * planes * lax.axis_size("brick"))
    return elementals_of(eigen, links, block_slot, factor)


def solution(mesh):
    return jax.shard_map(
        on_device,
        mesh=mesh,
        in_specs=(
            P(None, None, None, ("cuts", "brick"), None),
            P(None, None, None, None, ("cuts", "brick"), None),
            P(),
        ),
        out_specs=P(("cuts", "brick"), None, None),
        check_vma=False,
    )
```

```python
import functools
import math

import jax
import jax.numpy as jnp
from jax import lax
from jax.experimental import pallas as pl
from jax.experimental.pallas import tpu as pltpu
from jax.sharding import PartitionSpec as P

PB = 32
CAP = 4
LX = 8
LY = 64

LANES = 128
TILE = 8
GROUP = 32
ROWS = 16
AHEAD = 2
MESH = pl.DeviceIdType.MESH


def shifted_columns(row, column, forward):
    lanes = row.shape[-1]
    if forward:
        return jnp.where(
            column == LX - 1, pltpu.roll(row, LX - 1, 1), pltpu.roll(row, lanes - 1, 1)
        )
    return jnp.where(column == 0, pltpu.roll(row, lanes - LX + 1, 1), pltpu.roll(row, 1, 1))


def times_link(links, field, adjoint, totals):
    for row in range(3):
        for col in range(3):
            at = col * 3 + row if adjoint else row * 3 + col
            real, imag = links(at), links(9 + at)
            if adjoint:
                terms = (
                    real * field[col] + imag * field[3 + col],
                    real * field[3 + col] - imag * field[col],
                )
            else:
                terms = (
                    real * field[col] - imag * field[3 + col],
                    real * field[3 + col] + imag * field[col],
                )
            for part, term in zip((row, 3 + row), terms):
                totals[part] = term if totals[part] is None else totals[part] + term


def pair_diquarks(left, right):
    parts = [None] * 6
    for colour in range(3):
        first = (colour + 1) % 3
        second = (colour + 2) % 3
        common = left[6 + first] * right[second] - left[6 + second] * right[first]
        turned = left[first] * right[3 + second] - left[second] * right[3 + first]
        summed = left[3 + first] * right[6 + second] - left[3 + second] * right[6 + first]
        parts[colour] = common - summed
        parts[3 + colour] = common + turned
    return parts


ROW_TILE = 8
DOT_TILES = 16


def row_tiles(half):
    tiles = []
    count = half // ROW_TILE
    for side in range(2):
        for left in range(half - ROW_TILE):
            tiles += [(side, left, tile, 0) for tile in range(left // ROW_TILE + 1, count)]
        for tile in range(count):
            for shift in range(1, ROW_TILE // 2 + 1):
                tiles.append((side, None, tile, shift))
    return tiles


def stage_order(chunks):
    order = [(0, chunk) for chunk in range(min(3, chunks))]
    for chunk in range(3, chunks):
        order += [(1, chunk - 2), (0, chunk)]
    left = [chunk for chunk in range(chunks) if (1, chunk) not in order]
    return order + [(1, chunk) for chunk in left if chunk > 0] + [(1, 0)]


def bit_orders(levels):
    plain = list(range(levels))
    return [plain, plain] + [plain[:1] + plain[2:3] + plain[1:2] + plain[3:]] * 2


def whole_kernel(factor, slot_ref, eigen_in, link_in, out_ref, *scratch):
    levels = lax.axis_size("brick").bit_length() - 1
    (
        eigen_ref,
        link_ref,
        first_ref,
        near_halo,
        far_halo,
        lower_ref,
        wide_ref,
        field_ref,
        mixed_ref,
        quark_ref,
        low_ref,
        sum_ref,
        square_ref,
        turned_ref,
        pair_ref,
        inverse_ref,
        eigen_load,
        link_load,
        halo_send,
        halo_recv,
        link_send,
        link_recv,
        piece_send,
        piece_recv,
        *stages,
    ) = scratch
    held = stages[:levels]
    landed = stages[levels:]

    planes, chunks, _, vectors, _ = eigen_ref.shape
    count = lax.axis_size("brick")
    me = lax.axis_index("brick")
    above = lax.rem(me + 1, count)
    below = lax.rem(me + count - 1, count)
    bits = [lax.rem(me // (1 << level), 2) for level in range(levels)]
    partners = [me + (1 - 2 * bits[level]) * (1 << level) for level in range(levels)]

    barrier = pltpu.get_barrier_semaphore()
    for other in [below, above] + partners:
        pl.semaphore_signal(barrier, inc=1, device_id={"brick": other}, device_id_type=MESH)

    def load_links(axis, plane):
        return pltpu.make_async_copy(
            link_in.at[axis, :, plane], link_ref.at[axis, plane], link_load.at[axis, plane]
        )

    def load_eigen(plane, chunk, part):
        return pltpu.make_async_copy(
            eigen_in.at[:, part, plane, pl.ds(chunk * LANES, LANES)],
            eigen_ref.at[plane, chunk, part],
            eigen_load.at[plane, chunk, part],
        )

    axis_planes = [(axis, plane) for axis in (2, 0, 1) for plane in reversed(range(planes))]

    def start_eigen(chunk):
        for plane in range(planes):
            for part in range(6):
                load_eigen(plane, chunk, part).start()

    start_eigen(0)
    load_links(*axis_planes[0]).start()

    def wait_eigen(chunk):
        for plane in range(planes):
            for part in range(6):
                load_eigen(plane, chunk, part).wait()

    pl.semaphore_wait(barrier, 2 + levels)

    groups = vectors // GROUP

    def halo_copy(hop, side, chunk, group):
        source = (eigen_ref, first_ref)[hop]
        target = (near_halo, far_halo)[hop]
        rows = pl.ds(pl.multiple_of(group * GROUP, GROUP), GROUP)
        return pltpu.make_async_remote_copy(
            src_ref=source.at[planes - 1 if side == 0 else 0, chunk, :, rows],
            dst_ref=target.at[side, chunk, :, rows],
            send_sem=halo_send.at[hop, side, chunk, group],
            recv_sem=halo_recv.at[hop, side, chunk, group],
            device_id={"brick": above if side == 0 else below},
            device_id_type=MESH,
        )

    link_copy = pltpu.make_async_remote_copy(
        src_ref=link_ref.at[2, planes - 1],
        dst_ref=lower_ref,
        send_sem=link_send,
        recv_sem=link_recv,
        device_id={"brick": above},
        device_id_type=MESH,
    )
    order = stage_order(chunks)

    def stage_of(stage):
        hop, chunk = order[-1]
        for at, (other_hop, other_chunk) in enumerate(order[:-1]):
            hop = jnp.where(stage == at, other_hop, hop)
            chunk = jnp.where(stage == at, other_chunk, chunk)
        return hop, chunk

    for at, (hop, chunk) in enumerate(order[:AHEAD]):
        wait_eigen(chunk)
        for group in range(groups):
            for side in range(2):
                halo_copy(hop, side, chunk, group).start()
        if at == 0:
            load_links(2, planes - 1).wait()
            link_copy.start()
            for later in range(1, chunks):
                start_eigen(later)
            for axis, plane in axis_planes[1:]:
                load_links(axis, plane).start()

    for axis, plane in axis_planes[1:]:
        load_links(axis, plane).wait()
    for hop, chunk in order[AHEAD:]:
        if hop == 0:
            wait_eigen(chunk)

    def widen(direction, plane, block):
        for at in range(18):
            for chunk in range(chunks):
                wide_ref[direction, plane, chunk, at] = jnp.broadcast_to(
                    block[at : at + 1, chunk * LANES : (chunk + 1) * LANES], (TILE, LANES)
                )

    link_column = lax.broadcasted_iota(jnp.int32, link_ref.shape[2:], 1) % LX
    for plane in range(planes):
        along_x, along_y, along_z = (link_ref[axis, plane] for axis in range(3))
        widen(0, plane, along_x)
        widen(1, plane, shifted_columns(along_x, link_column, False))
        widen(2, plane, along_y)
        widen(3, plane, pltpu.roll(along_y, LX, 1))
        widen(4, plane, along_z)
        if plane > 0:
            widen(5, plane, link_ref[2, plane - 1])

    blocks = slot_ref.shape[0]

    def find_slots(group, carry):
        slots = [group * CAP + at for at in range(CAP)]

        def look(block, found):
            named = slot_ref[block]
            return [jnp.where(named == slot, block, last) for slot, last in zip(slots, found)]

        found = lax.fori_loop(0, blocks, look, [blocks] * CAP, unroll=True)
        for slot, block in zip(slots, found):
            inverse_ref[slot] = block
        return carry

    lax.fori_loop(0, count, find_slots, 0)
    sum_ref[...] = jnp.zeros_like(sum_ref)

    link_copy.wait_recv()
    widen(5, 0, lower_ref[...])

    lane = lax.broadcasted_iota(jnp.int32, (ROWS, LANES), 1)
    column = lane % LX

    def hop_tile(source, halo, chunk, plane, at):
        rows = pl.ds(pl.multiple_of(at * ROWS, ROWS), ROWS)
        after = lax.rem(chunk + 1, chunks)
        before = lax.rem(chunk + chunks - 1, chunks)
        middle = [source[plane, chunk, part, rows, :] for part in range(6)]
        totals = [None] * 6

        def links(direction):
            def link(at):
                return jnp.concatenate([wide_ref[direction, plane, chunk, at]] * (ROWS // TILE), 0)

            return link

        field = [shifted_columns(cell, column, True) for cell in middle]
        times_link(links(0), field, False, totals)
        field = [shifted_columns(cell, column, False) for cell in middle]
        times_link(links(1), field, True, totals)
        field = [
            pltpu.roll(
                jnp.where(lane < LX, source[plane, after, part, rows, :], middle[part]),
                LANES - LX,
                1,
            )
            for part in range(6)
        ]
        times_link(links(2), field, False, totals)
        field = [
            pltpu.roll(
                jnp.where(lane < LANES - LX, middle[part], source[plane, before, part, rows, :]),
                LX,
                1,
            )
            for part in range(6)
        ]
        times_link(links(3), field, True, totals)
        if plane + 1 < planes:
            field = [source[plane + 1, chunk, part, rows, :] for part in range(6)]
        else:
            field = [halo[1, chunk, part, rows, :] for part in range(6)]
        times_link(links(4), field, False, totals)
        if plane > 0:
            field = [source[plane - 1, chunk, part, rows, :] for part in range(6)]
        else:
            field = [halo[0, chunk, part, rows, :] for part in range(6)]
        times_link(links(5), field, True, totals)
        return rows, totals

    tiles_in = GROUP // ROWS

    def send_later(stage, group):
        for hop in range(2):
            later_hop, later_chunk = stage_of(stage + AHEAD)

            @pl.when(jnp.logical_and(stage + AHEAD < len(order), later_hop == hop))
            def _():
                for side in range(2):
                    halo_copy(hop, side, later_chunk, group).start()

    def first_stage(stage, chunk):
        def one_group(group, carry):
            for side in range(2):
                halo_copy(0, side, chunk, group).wait_recv()

            def one_tile(at, inner):
                for plane in range(planes):
                    rows, values = hop_tile(eigen_ref, near_halo, chunk, plane, at)
                    for part in range(6):
                        first_ref[plane, chunk, part, rows, :] = values[part] * (1.0 / 6.0)
                return inner

            for at in range(tiles_in):
                one_tile(group * tiles_in + at, 0)
            send_later(stage, group)
            return carry

        lax.fori_loop(0, groups, one_group, 0)

    half = vectors // 2
    tiles = row_tiles(half)

    def elementals(plane, carry):
        for colour in range(3):
            real = field_ref[plane, colour]
            imag = field_ref[plane, 3 + colour]
            mixed_ref[colour] = imag - real
            mixed_ref[3 + colour] = imag + real
            real_low = real.astype(jnp.bfloat16)
            imag_low = imag.astype(jnp.bfloat16)
            real_at = slice(colour * LANES, (colour + 1) * LANES)
            imag_at = slice((3 + colour) * LANES, (4 + colour) * LANES)
            low_ref[:vectors, real_at] = real_low
            low_ref[:vectors, imag_at] = -imag_low
            low_ref[vectors:, real_at] = imag_low
            low_ref[vectors:, imag_at] = real_low

        lefts = {}

        def one_tile(side, left_at, tile, shift):
            rows = slice(side * half + tile * ROW_TILE, side * half + (tile + 1) * ROW_TILE)
            right = [field_ref[plane, colour, rows, :] for colour in range(3)]
            right += [mixed_ref[part, rows, :] for part in range(6)]
            if left_at is None:
                left = [field_ref[plane, part, rows, :] for part in range(6)] + right[6:]
                right = [pltpu.roll(cells, ROW_TILE - shift, 0) for cells in right]
                return pair_diquarks(left, right)
            left_at += side * half

            def spread(cells):
                return jnp.broadcast_to(cells, (ROW_TILE, LANES))

            if left_at not in lefts:
                lefts.clear()
                at = slice(left_at, left_at + 1)
                left = [spread(field_ref[plane, part, at, :]) for part in range(6)]
                left += [spread(mixed_ref[3 + colour, at, :]) for colour in range(3)]
                lefts[left_at] = left
            left = lefts[left_at]
            return pair_diquarks(left, right)

        for from_tile in range(0, len(tiles), DOT_TILES):
            to_tile = min(from_tile + DOT_TILES, len(tiles))
            for at in range(from_tile, to_tile, 2):
                upper = one_tile(*tiles[at])
                lower = one_tile(*tiles[at + 1])
                for part in range(6):
                    quark_ref[
                        at * ROW_TILE : (at + 2) * ROW_TILE, part * LANES : (part + 1) * LANES
                    ] = jnp.concatenate([upper[part], lower[part]], 0).astype(jnp.bfloat16)
            rows = slice(from_tile * ROW_TILE, to_tile * ROW_TILE)
            sum_ref[rows, :] += lax.dot_general(
                quark_ref[rows, :],
                low_ref[...],
                (((1,), (1,)), ((), ())),
                preferred_element_type=jnp.float32,
            )
        return carry

    def last_stage(stage, chunk):
        def one_group(group, carry):
            for side in range(2):
                halo_copy(1, side, chunk, group).wait_recv()
            send_later(stage, group)

            def one_tile(at, inner):
                for plane in range(planes):
                    rows, values = hop_tile(first_ref, far_halo, chunk, plane, at)
                    for part in range(6):
                        field_ref[plane, part, rows, :] = (
                            (1.0 / 3.0) * values[part] - eigen_ref[plane, chunk, part, rows, :]
                        )
                return inner

            for at in range(tiles_in):
                one_tile(group * tiles_in + at, 0)
            return carry

        lax.fori_loop(0, groups, one_group, 0)
        lax.fori_loop(0, planes, elementals, 0)

    def one_stage(stage, carry):
        hop, chunk = stage_of(stage)

        @pl.when(hop == 0)
        def _():
            first_stage(stage, chunk)

        @pl.when(hop == 1)
        def _():
            last_stage(stage, chunk)

        return carry

    lax.fori_loop(0, len(order), one_stage, 0)

    def put_pairs(pair_at, cells):
        done = 0
        while done < cells.shape[0]:
            block, row = divmod(pair_at + done, PB)
            some = min(PB - row, cells.shape[0] - done)
            pair_ref[block, row : row + some, :] = cells[done : done + some]
            done += some

    def first_pair(left):
        return left * (2 * vectors - left - 1) // 2

    def square_rows(side, left, row, rows):
        start = (side * half + left) * half + row
        return slice(start, start + rows)

    def square_put(side, left, row, cells, left_step, row_step):
        start = (side * half + left) * half + row
        step = left_step * half + row_step
        square_ref[pl.ds(start, cells.shape[0], stride=step), :] = cells

    for at, (side, left, tile, shift) in enumerate(tiles):
        cells = sum_ref[at * ROW_TILE : (at + 1) * ROW_TILE, :] * factor
        row = tile * ROW_TILE
        if shift == 0:
            square_ref[square_rows(side, left, row, ROW_TILE), :] = cells
            square_put(side, row, left, -cells, 1, 0)
        else:
            upper, lower = cells[: ROW_TILE - shift], cells[ROW_TILE - shift :]
            square_put(side, row, row + shift, upper, 1, 1)
            square_put(side, row + shift, row, -upper, 1, 1)
            square_put(side, row + ROW_TILE - shift, row, lower, 1, 1)
            square_put(side, row, row + ROW_TILE - shift, -lower, 1, 1)
    for side in range(2):
        for row in range(0, half, ROW_TILE):
            nothing = jnp.zeros((ROW_TILE, 2 * vectors), jnp.float32)
            square_put(side, row, row, nothing, 1, 1)
        for left in range(half - 1):
            rows = square_rows(side, left, left + 1, half - 1 - left)
            put_pairs(first_pair(side * half + left), square_ref[rows, :])

    together = 2 * vectors // half
    apart = half // together
    for at in range(apart):
        stack = [square_ref[square_rows(1, at + apart * up, 0, half), :] for up in range(together)]
        turned_ref[pl.ds(at, 2 * vectors, stride=apart), :] = jnp.concatenate(stack, 0).T
    part = lax.broadcasted_iota(jnp.int32, (half, 2 * vectors), 1) // half
    for quad in range(apart):
        mine = square_ref[square_rows(0, quad * together, 0, together * half), :].T
        near_real = -mine[half:vectors]
        near_imag = -mine[vectors + half :]
        for up in range(together):
            left = quad * together + up

            def far(row):
                cells = turned_ref[row * apart : (row + 1) * apart, :]
                return jnp.concatenate(
                    [
                        pltpu.roll(cells, (2 * half * (row >= vectors) + half - half * at) % LANES, 1)
                        for at in range(together)
                    ],
                    0,
                )

            def near(cells, to):
                return pltpu.roll(cells, (to - up) * half % LANES, 1)

            cells = jnp.where(part == 0, near(near_real, 0), near(near_imag, 2))
            cells = jnp.where(part == 1, far(left), cells)
            cells = jnp.where(part == 3, far(vectors + left), cells)
            put_pairs(first_pair(left) + half - 1 - left, cells)
    pair_ref[blocks] = jnp.zeros((PB, 2 * vectors), jnp.float32)

    orders = bit_orders(levels)

    def piece_copy(level, piece):
        axis = orders[piece][level]
        return pltpu.make_async_remote_copy(
            src_ref=held[level].at[piece, 1 - bits[axis]],
            dst_ref=landed[level].at[piece],
            send_sem=piece_send.at[level, piece],
            recv_sem=piece_recv.at[level, piece],
            device_id={"brick": partners[axis]},
            device_id_type=MESH,
        )

    schedule = [0, 2, 1, 3]
    for piece in schedule:
        for device in range(count):
            at = tuple((device >> axis) & 1 for axis in orders[piece])
            held[0][(piece,) + at] = pair_ref[inverse_ref[device * CAP + piece]]
        piece_copy(0, piece).start()
    for level in range(levels):
        for piece in schedule:
            piece_copy(level, piece).wait_recv()
            total = held[level][piece, bits[orders[piece][level]]] + landed[level][piece]
            if level + 1 < levels:
                held[level + 1][piece] = total
                piece_copy(level + 1, piece).start()
            else:
                out_ref[piece] = total
    link_copy.wait_send()
    for hop in range(2):
        for chunk in range(chunks):
            for group in range(groups):
                for side in range(2):
                    halo_copy(hop, side, chunk, group).wait_send()
    for level in range(levels):
        for piece in schedule:
            piece_copy(level, piece).wait_send()


def elementals_of(eigen, links, block_slot, factor):
    vectors, parts, planes, sites = eigen.shape
    chunks, lanes = sites // LANES, LANES
    devices = lax.axis_size("brick")
    levels = devices.bit_length() - 1
    tile_rows = len(row_tiles(vectors // 2)) * ROW_TILE
    halo = pltpu.VMEM((2, chunks, parts, vectors, lanes), jnp.float32)
    vmem = pl.BlockSpec(memory_space=pltpu.VMEM)
    stay = pl.BlockSpec(memory_space=pl.ANY)
    copies = pltpu.SemaphoreType.DMA((2, 2, chunks, vectors // GROUP))
    pieces = pltpu.SemaphoreType.DMA((levels, CAP))

    def stage(depth):
        return pltpu.VMEM((CAP,) + (2,) * depth + (PB, 2 * vectors), jnp.float32)

    return pl.pallas_call(
        functools.partial(whole_kernel, factor),
        in_specs=[pl.BlockSpec(memory_space=pltpu.SMEM), stay, stay],
        out_specs=vmem,
        out_shape=jax.ShapeDtypeStruct((CAP, PB, 2 * vectors), jnp.float32),
        scratch_shapes=[
            pltpu.VMEM((planes, chunks, parts, vectors, lanes), jnp.float32),
            pltpu.VMEM((3, planes, 18, sites), jnp.float32),
            pltpu.VMEM((planes, chunks, parts, vectors, lanes), jnp.float32),
            halo,
            halo,
            pltpu.VMEM((18, sites), jnp.float32),
            pltpu.VMEM((6, planes, chunks, 18, TILE, lanes), jnp.float32),
            pltpu.VMEM((planes, 6, vectors, lanes), jnp.float32),
            pltpu.VMEM((6, vectors, lanes), jnp.float32),
            pltpu.VMEM((tile_rows, 6 * lanes), jnp.bfloat16),
            pltpu.VMEM((2 * vectors, 6 * lanes), jnp.bfloat16),
            pltpu.VMEM((tile_rows, 2 * vectors), jnp.float32),
            pltpu.VMEM((vectors * vectors // 2, 2 * vectors), jnp.float32),
            pltpu.VMEM((vectors // 4 * vectors, 2 * vectors), jnp.float32),
            pltpu.VMEM((block_slot.shape[0] + 1, PB, 2 * vectors), jnp.float32),
            pltpu.SMEM((CAP * devices,), jnp.int32),
            pltpu.SemaphoreType.DMA((planes, chunks, 6)),
            pltpu.SemaphoreType.DMA((3, planes)),
            copies,
            copies,
            pltpu.SemaphoreType.DMA,
            pltpu.SemaphoreType.DMA,
            pieces,
            pieces,
        ]
        + [stage(levels - level) for level in range(levels)]
        + [stage(levels - 1 - level) for level in range(levels)],
        compiler_params=pltpu.CompilerParams(
            collective_id=0, has_side_effects=True, vmem_limit_bytes=60 << 20
        ),
        name="elementals",
    )(block_slot, eigen, links)


def on_device(eigen_vectors, link_field, block_slot):
    vectors = eigen_vectors.shape[0]
    planes, sites = eigen_vectors.shape[3:]
    eigen = eigen_vectors.reshape(vectors, 6, planes, sites)
    links = link_field.reshape(3, 18, planes, sites)
    factor = 1.0 / math.sqrt(3.0 * LX * LY * planes * lax.axis_size("brick"))
    return elementals_of(eigen, links, block_slot, factor)


def solution(mesh):
    return jax.shard_map(
        on_device,
        mesh=mesh,
        in_specs=(
            P(None, None, None, ("cuts", "brick"), None),
            P(None, None, None, None, ("cuts", "brick"), None),
            P(),
        ),
        out_specs=P(("cuts", "brick"), None, None),
        check_vma=False,
    )
```
